128 devices in a mesh: src: 8 (over y, core), tgt: 16 (over z, x).
Axes of the slice: x: 4, y: 4, z: 4, core: 2. Of those that a mesh axis runs over, the one named last changes fastest.
Arguments:
- src_vel: bfloat16 [2, 48, 524288], P(None, None, ('src', 'tgt')), may hold values from -6 to 6
- angle: float32 [524288], P(('src', 'tgt')), may hold values from -3.140625 to 3.140625
- src_block: int32 [8, 16, 16, 8], P('src', 'tgt'), may hold values from 0 to 31
- tgt_block: int32 [8, 16, 16, 8], P('src', 'tgt'), may hold values from 0 to 31
- send_count: int32 [8, 16, 16], P('src', 'tgt'), may hold values from 0 to 8, as said below
- intersection: bfloat16 [8, 16, 16, 8, 128, 128], P('src', 'tgt'), may hold values from -0.375 to 0.375
- eofs: bfloat16 [512, 2, 524288], P(None, None, ('src', 'tgt')), may hold values from -0.0234375 to 0.0234375
Outputs:
- remapped: bfloat16 [2, 48, 524288], P(None, None, ('src', 'tgt'))
- pcs: float32 [48, 512], P(None, 'tgt')
The draws below stay inside these ranges and needn't reach their ends.
Inputs may be any that keep to these rules, and one draw needn't show every extreme that they name: `src_block`: indices of the sending device's own source blocks. `tgt_block`: indices of the receiving device's target blocks. `send_count`: in every tile row, one receiver column gets 8 live slots from every sender of the row.
All inputs are finite; a program needn't handle non-finite values.
Results may differ from the reference program's by a relative error of at most 0.0058.
Values may be sent and summed in bfloat16 or wider, within the bound.
No kernel may reach another device: no remote copies, remote signals or barrier semaphores. Data moves between devices by JAX's collectives and lax.ppermute only.
A program may use at most 64 MiB of HBM per device.

```python
import jax
import jax.numpy as jnp
from jax import lax

BLK = 128
SB = 32
TB = 32
CAP = 8
K = 512
TL = 48
SCELLS = 524288
TCELLS = 524288
N_SRC = 8
N_TGT = 16


def draw_send_count(key, part):
    first_key, second_key = jax.random.split(jax.random.fold_in(key, 11))
    base = jax.random.randint(first_key, (N_SRC, N_TGT, N_TGT), 0, CAP + 1)
    full_col = jax.random.randint(second_key, (N_SRC, 1, 1), 0, N_TGT)
    column = lax.broadcasted_iota(jnp.int32, (N_SRC, N_TGT, N_TGT), 2)
    return jnp.where(column == full_col, CAP, base).astype(jnp.int32)


def set_ends(drawn, own_key, smallest, top_value):
    shape = drawn.shape
    spot = [jax.random.randint(jax.random.fold_in(own_key, axis), (), 0, shape[axis]) for axis in range(len(shape))]
    drawn = drawn.at[tuple(spot)].set(smallest)
    longest = shape.index(max(shape))
    spot[longest] = (spot[longest] + 1) % shape[longest]
    return drawn.at[tuple(spot)].set(top_value)


def with_spikes(values, own_key, source, target, shards_of, factor):
    def block_of(dim):
        return (jnp.arange(values.shape[dim]) // (values.shape[dim] // shards_of)).reshape((-1,) + (1,) * (values.ndim - 1 - dim))

    near = jax.random.permutation(own_key, shards_of)[block_of(target)]
    far = (block_of(target) + shards_of // 2) % shards_of
    return jnp.where((block_of(source) == near) | (block_of(source) == far), factor * values, values)


def level_of(own_key, extent, pieces, least, top_value):
    gain, own = 1.0, jax.random.fold_in(own_key, 6)
    for dim, parts in pieces:
        steps = jnp.exp(jax.random.uniform(jax.random.fold_in(own, dim), (parts,), jnp.float32, least / len(pieces), top_value / len(pieces)))
        gain = gain * jnp.repeat(steps, extent[dim] // parts).reshape([-1 if axis == dim else 1 for axis in range(len(extent))])
    return gain


def normal_values(own_key, extent, scale, bound, cuts=(), kind=jnp.bfloat16):
    array = jax.random.normal(own_key, extent, jnp.float32) * scale
    if len(cuts) > 0:
        array = level_of(own_key, extent, cuts, -0.22, 0.18) * array
    return jnp.clip(array, min=-bound, max=bound).astype(kind)


def heavy_noise(stream_key, shape, spread, reach, cuts, heavy, held_as=jnp.bfloat16):
    values = spread * jax.random.normal(stream_key, shape, jnp.float32)
    if cuts:
        values = values * level_of(stream_key, shape, cuts, -0.22, 0.18)
    return jnp.clip(with_spikes(values, jax.random.fold_in(stream_key, 3), *heavy), -reach, reach).astype(held_as)


def setup_inputs(seed: int = 0) -> dict:
    key_of = jax.random.split(jax.random.key(seed), 8)
    src_vel = normal_values(key_of[0], (2, TL, SCELLS), 1.0, 6.0, ((2, 128),))
    angle = jnp.clip(jax.random.uniform(key_of[1], (SCELLS,), jnp.float32, -3.140625, 3.140625), -3.140625, 3.140625)
    src_block = set_ends(jax.random.randint(key_of[2], (N_SRC, N_TGT, N_TGT, CAP), 0, SB), jax.random.fold_in(key_of[2], 1), 0, SB - 1).astype(jnp.int32)
    tgt_block = set_ends(jax.random.randint(key_of[3], (N_SRC, N_TGT, N_TGT, CAP), 0, TB), jax.random.fold_in(key_of[3], 1), 0, TB - 1).astype(jnp.int32)
    send_count = draw_send_count(jax.random.fold_in(key_of[7], 71), 0)
    intersection = normal_values(key_of[5], (N_SRC, N_TGT, N_TGT, CAP, BLK, BLK), (2 * BLK) ** -0.5, 0.375, ((0, 8), (1, 16)))
    eofs = heavy_noise(key_of[6], (K, 2, TCELLS), (2 * TCELLS) ** -0.5, 0.0234375, ((2, 128),), (2, 0, 128, 5.5))
    return dict(src_vel=src_vel, angle=angle, src_block=src_block, tgt_block=tgt_block, send_count=send_count, intersection=intersection, eofs=eofs)


def remap_row(rotated_row, ids_src, ids_tgt, counts, weights):
    tgt_count = ids_src.shape[0]
    slot_cap = ids_src.shape[2]
    take_index = ids_src.reshape(1, 1, tgt_count, tgt_count * slot_cap, 1).astype(jnp.int32)
    blocks = jnp.take_along_axis(rotated_row, take_index, axis=3)
    weight_rows = weights.reshape(tgt_count, tgt_count * slot_cap, BLK, BLK).astype(jnp.float32)
    contribs = jnp.einsum('ctspi,spij->spctj', blocks.astype(jnp.float32), weight_rows).astype(jnp.bfloat16)
    slot_iota = jnp.arange(slot_cap, dtype=jnp.int32)
    live_slot = slot_iota[None, None, :] < counts[:, :, None]
    target_id = jnp.where(live_slot, ids_tgt, TB)
    onehot = (target_id[..., None] == jnp.arange(TB, dtype=jnp.int32)).astype(jnp.float32)
    contrib_six = contribs.reshape(tgt_count, tgt_count, slot_cap, 2, TL, BLK).astype(jnp.float32)
    return jnp.einsum('sdcb,sdcxyj->xydbj', onehot, contrib_six)


def reference(src_vel, angle, src_block, tgt_block, send_count, intersection, eofs):
    velocity = src_vel.astype(jnp.float32).reshape(2, TL, N_SRC, N_TGT, SB, BLK)
    fold_row = velocity[:, :, N_SRC - 1, :, SB - 1, :]
    mirror = fold_row[:, :, ::-1, ::-1]
    velocity = velocity.at[:, :, N_SRC - 1, :, SB - 1, :].set(0.5 * (fold_row - mirror))
    angles = angle.reshape(N_SRC, N_TGT, SB, BLK)
    cosine = jnp.cos(angles)
    sine_part = jnp.sin(angles)
    zonal = velocity[0]
    meridional = velocity[1]
    eastward = cosine * zonal - sine_part * meridional
    northward = sine_part * zonal + cosine * meridional
    rotated = jnp.stack([eastward, northward]).astype(jnp.bfloat16)
    rot_rows = jnp.moveaxis(rotated, 2, 0)

    def one_row(packed):
        return remap_row(packed[0], packed[1], packed[2], packed[3], packed[4])

    summed = lax.map(one_row, (rot_rows, src_block, tgt_block, send_count, intersection))
    summed = jnp.moveaxis(summed, 0, 2)
    remapped = summed.reshape(2, TL, TCELLS).astype(jnp.bfloat16)
    field_rows = jnp.transpose(remapped, (1, 0, 2)).reshape(TL, 2 * TCELLS)
    eof_rows = eofs.reshape(K, 2 * TCELLS)
    pcs = lax.dot_general(field_rows, eof_rows, (((1,), (1,)), ((), ())), preferred_element_type=jnp.float32)
    return remapped, pcs
```

```python
import jax
import jax.numpy as jnp
from jax import lax
from jax.experimental import pallas as pl
from jax.experimental.pallas import tpu as pltpu
from jax.sharding import PartitionSpec as P

BLK = 128
ID_ROWS = 16
W_CHUNK = 8
EOF_PARTS = 8
SHIFT = 64


def in_hbm(x):
    return pltpu.with_memory_space_constraint(x, pltpu.HBM)


def contribution_kernel(codes, vel_hbm, angle_ref, mirror_ref, w_hbm, out_hbm, vel, w, rot, out, vel_sem, w_sem, out_sem):
    components, rows, cells = vel.shape
    blocks = cells // BLK
    slots = w.shape[0]
    peers, peer_rows, _ = out.shape
    cap = slots // peers
    chunks = slots // W_CHUNK
    height = components * rows

    def w_copy(i):
        part = pl.ds(i * W_CHUNK, W_CHUNK)
        return pltpu.make_async_copy(w_hbm.at[part], w.at[part], w_sem.at[i])

    def out_copy(i):
        return pltpu.make_async_copy(out.at[i], out_hbm.at[i], out_sem.at[i])

    vel_copy = pltpu.make_async_copy(vel_hbm, vel, vel_sem)
    vel_copy.start()
    for i in range(chunks):
        w_copy(i).start()
    cosine = jnp.cos(angle_ref[...])
    sine = jnp.sin(angle_ref[...])
    lane = lax.broadcasted_iota(jnp.int32, (ID_ROWS, BLK), 1)
    for d in range(peers):
        ids = jnp.full((ID_ROWS, BLK), blocks, jnp.int32)
        for j in range(cap):
            ids = jnp.where(lane == j, codes[d * cap + j] % SHIFT, ids)
        out[d, cap * height :, :] = ids.astype(jnp.float32).astype(jnp.bfloat16)
    top = lax.axis_index("src") == lax.axis_size("src") - 1
    own_share = jnp.where(top, 0.5, 1.0).astype(jnp.float32)
    mirror_share = jnp.where(top, 0.5, 0.0).astype(jnp.float32)
    vel_copy.wait()
    for b in range(blocks):
        x = vel[0, :, b * BLK : (b + 1) * BLK].astype(jnp.float32)
        y = vel[1, :, b * BLK : (b + 1) * BLK].astype(jnp.float32)
        if b == blocks - 1:
            x = own_share * x - mirror_share * mirror_ref[0].astype(jnp.float32)
            y = own_share * y - mirror_share * mirror_ref[1].astype(jnp.float32)
        c = cosine[b : b + 1, :]
        s = sine[b : b + 1, :]
        rot[b, :rows, :] = (c * x - s * y).astype(jnp.bfloat16)
        rot[b, rows:, :] = (s * x + c * y).astype(jnp.bfloat16)

    for d in range(peers):
        for i in range(d * cap // W_CHUNK, (d + 1) * cap // W_CHUNK):
            w_copy(i).wait()
        for j in range(cap):
            p = d * cap + j
            block = rot[codes[p] // SHIFT]
            product = jnp.dot(block, w[p], preferred_element_type=jnp.float32)
            out[d, j * height : (j + 1) * height, :] = product.astype(jnp.bfloat16)
        out_copy(d).start()
    for d in range(peers):
        out_copy(d).wait()


def contributions(codes, src_vel, angle, mirror, weights, peers):
    components, rows, cells = src_vel.shape
    slots = weights.shape[0]
    blocks = cells // BLK
    height = components * rows
    peer_rows = slots // peers * height + ID_ROWS
    return pl.pallas_call(
        contribution_kernel,
        out_shape=jax.ShapeDtypeStruct((peers, peer_rows, BLK), jnp.bfloat16),
        in_specs=[
            pl.BlockSpec(memory_space=pltpu.SMEM),
            pl.BlockSpec(memory_space=pltpu.HBM),
            pl.BlockSpec(memory_space=pltpu.VMEM),
            pl.BlockSpec(memory_space=pltpu.VMEM),
            pl.BlockSpec(memory_space=pltpu.HBM),
        ],
        out_specs=pl.BlockSpec(memory_space=pltpu.HBM),
        scratch_shapes=[
            pltpu.VMEM(src_vel.shape, jnp.bfloat16),
            pltpu.VMEM(weights.shape, jnp.bfloat16),
            pltpu.VMEM((blocks, height, BLK), jnp.bfloat16),
            pltpu.VMEM((peers, peer_rows, BLK), jnp.bfloat16),
            pltpu.SemaphoreType.DMA,
            pltpu.SemaphoreType.DMA((slots // W_CHUNK,)),
            pltpu.SemaphoreType.DMA((peers,)),
        ],
        compiler_params=pltpu.CompilerParams(vmem_limit_bytes=24 << 20),
        name="contributions",
    )(codes, in_hbm(src_vel), angle.reshape(blocks, BLK), mirror, in_hbm(weights))


def remap_kernel(recv, eof_hbm, out_ref, pcs_ref, eof, acc, ids_vmem, ids_smem, sem, eof_sem):
    components, rows, cells = out_ref.shape
    blocks = cells // BLK
    peers, peer_rows, _ = recv.shape
    height = components * rows
    cap = (peer_rows - ID_ROWS) // height
    width = cells // EOF_PARTS

    def eof_copy(i):
        part = (slice(None), slice(None), pl.ds(i * width, width))
        return pltpu.make_async_copy(eof_hbm.at[part], eof.at[i], eof_sem.at[i])

    for i in range(EOF_PARTS):
        eof_copy(i).start()
    for s in range(peers):
        ids = recv[s, cap * height : cap * height + ID_ROWS, :].astype(jnp.float32).astype(jnp.int32)
        ids_vmem[s : s + 1, :] = ids[:1, :]
    copy = pltpu.make_async_copy(ids_vmem, ids_smem, sem)
    copy.start()
    acc[...] = jnp.zeros_like(acc)
    copy.wait()

    def sender(s, carry):
        for j in range(cap):
            start = pl.multiple_of(ids_smem[s, j] * height, height)
            part = recv[s, j * height : (j + 1) * height, :].astype(jnp.float32)
            acc[pl.ds(start, height), :] += part
        return carry

    lax.fori_loop(0, peers, sender, 0)
    for b in range(blocks):
        total = acc[b * height : (b + 1) * height, :].astype(jnp.bfloat16)
        for c in range(components):
            out_ref[c, :, b * BLK : (b + 1) * BLK] = total[c * rows : (c + 1) * rows, :]
    result = 0.0
    for i in range(EOF_PARTS):
        eof_copy(i).wait()
        for c in range(components):
            result += lax.dot_general(
                eof[i, c],
                out_ref[c, :, i * width : (i + 1) * width],
                (((1,), (1,)), ((), ())),
                preferred_element_type=jnp.float32,
            )
    pcs_ref[...] = result


def remap(received, eofs, rows):
    components, modes, cells = eofs.shape
    peers = received.shape[0]
    height = components * rows
    return pl.pallas_call(
        remap_kernel,
        out_shape=(
            jax.ShapeDtypeStruct((components, rows, cells), jnp.bfloat16),
            jax.ShapeDtypeStruct((modes, rows), jnp.float32),
        ),
        in_specs=[pl.BlockSpec(memory_space=pltpu.VMEM), pl.BlockSpec(memory_space=pltpu.HBM)],
        out_specs=(pl.BlockSpec(memory_space=pltpu.VMEM),) * 2,
        scratch_shapes=[
            pltpu.VMEM((EOF_PARTS, components, modes, cells // EOF_PARTS), jnp.bfloat16),
            pltpu.VMEM(((cells // BLK + 1) * height, BLK), jnp.float32),
            pltpu.VMEM((peers, BLK), jnp.int32),
            pltpu.SMEM((peers, BLK), jnp.int32),
            pltpu.SemaphoreType.DMA,
            pltpu.SemaphoreType.DMA((EOF_PARTS,)),
        ],
        compiler_params=pltpu.CompilerParams(vmem_limit_bytes=32 << 20),
        name="remap",
    )(received, in_hbm(eofs))


def per_device(src_vel, angle, src_block, tgt_block, send_count, intersection, eofs):
    components, rows, cells = src_vel.shape
    src_count = lax.axis_size("src")
    tgt_count = lax.axis_size("tgt")
    cap = src_block.shape[3]
    slots = tgt_count * cap
    blocks = eofs.shape[2] // BLK
    edge = src_vel[:, :, cells - BLK :][:, :, ::-1]
    top = (src_count - 1) * tgt_count
    mirror = lax.ppermute(
        edge, ("src", "tgt"), [(top + t, top + tgt_count - 1 - t) for t in range(tgt_count)]
    )
    live = lax.broadcasted_iota(jnp.int32, (1, 1, tgt_count, cap), 3) < send_count[..., None]
    codes = (src_block * SHIFT + jnp.where(live, tgt_block, blocks)).reshape(slots)
    weights = intersection.reshape(slots, BLK, BLK)
    contribs = contributions(codes, src_vel, angle, mirror, weights, tgt_count)
    received = lax.all_to_all(contribs, "tgt", split_axis=0, concat_axis=0, tiled=True)
    remapped, partial = remap(received, jnp.swapaxes(eofs, 0, 1), rows)
    modes = partial.shape[0] // tgt_count
    pieces = partial.reshape(tgt_count, 2, modes // 2, rows)
    pieces = jnp.concatenate([pieces[:, 0], pieces[:, 1]], axis=-1)
    column = jnp.sum(lax.all_to_all(pieces, "tgt", 0, 0, tiled=True), axis=0)
    everyone = jnp.broadcast_to(column[None], (src_count, *column.shape))
    total = jnp.sum(lax.all_to_all(everyone, "src", 0, 0, tiled=True), axis=0)
    pcs = jnp.concatenate([total[:, :rows], total[:, rows:]], axis=0).T
    return remapped, pcs


def solution(mesh):
    return jax.shard_map(
        per_device,
        mesh=mesh,
        in_specs=(
            P(None, None, ("src", "tgt")),
            P(("src", "tgt")),
            P("src", "tgt", None, None),
            P("src", "tgt", None, None),
            P("src", "tgt", None),
            P("src", "tgt", None, None, None, None),
            P(None, None, ("src", "tgt")),
        ),
        out_specs=(P(None, None, ("src", "tgt")), P(None, "tgt")),
        check_vma=False,
    )
```

```python
import jax
import jax.numpy as jnp
from jax import lax
from jax.experimental import pallas as pl
from jax.experimental.pallas import tpu as pltpu
from jax.sharding import PartitionSpec as P

BLK = 128
ID_ROWS = 16
W_CHUNK = 8
EOF_PARTS = 2


def in_hbm(x):
    return pltpu.with_memory_space_constraint(x, pltpu.HBM)


def contribution_kernel(src_ids, tgt_ids, counts, vel_hbm, angle_hbm, mirror_ref, w_hbm, out, vel, angle, w, rot, vel_sem, angle_sem, w_sem):
    components, rows, cells = vel.shape
    blocks = cells // BLK
    slots = w.shape[0]
    peers, peer_rows, _ = out.shape
    cap = slots // peers
    chunks = slots // W_CHUNK
    height = components * rows

    def w_copy(i):
        part = pl.ds(i * W_CHUNK, W_CHUNK)
        return pltpu.make_async_copy(w_hbm.at[part], w.at[part], w_sem.at[i])

    angle_copy = pltpu.make_async_copy(angle_hbm, angle, angle_sem)
    angle_copy.start()
    vel_copy = pltpu.make_async_copy(vel_hbm, vel, vel_sem)
    vel_copy.start()
    for i in range(chunks):
        w_copy(i).start()
    lane = lax.broadcasted_iota(jnp.int32, (ID_ROWS, BLK), 1)
    for d in range(peers):
        ids = jnp.full((ID_ROWS, BLK), blocks, jnp.int32)
        for j in range(cap):
            ids = jnp.where(lane == j, jnp.where(j < counts[d], tgt_ids[j, d], blocks), ids)
        out[d, cap * height :, :] = ids.astype(jnp.float32).astype(jnp.bfloat16)
    top = lax.axis_index("src") == lax.axis_size("src") - 1
    own_share = jnp.where(top, 0.5, 1.0).astype(jnp.float32)
    mirror_share = jnp.where(top, 0.5, 0.0).astype(jnp.float32)
    angle_copy.wait()
    cosine = jnp.cos(angle[...])
    sine = jnp.sin(angle[...])
    vel_copy.wait()
    for b in range(blocks):
        x = vel[0, :, b * BLK : (b + 1) * BLK].astype(jnp.float32)
        y = vel[1, :, b * BLK : (b + 1) * BLK].astype(jnp.float32)
        if b == blocks - 1:
            x = own_share * x - mirror_share * mirror_ref[0].astype(jnp.float32)
            y = own_share * y - mirror_share * mirror_ref[1].astype(jnp.float32)
        c = cosine[b : b + 1, :]
        s = sine[b : b + 1, :]
        rot[b, :rows, :] = (c * x - s * y).astype(jnp.bfloat16)
        rot[b, rows:, :] = (s * x + c * y).astype(jnp.bfloat16)

    for d in range(peers):
        for i in range(d * cap // W_CHUNK, (d + 1) * cap // W_CHUNK):
            w_copy(i).wait()
        for j in range(cap):
            p = d * cap + j
            block = rot[src_ids[j, d]]
            product = jnp.dot(block, w[p], preferred_element_type=jnp.float32)
            out[d, j * height : (j + 1) * height, :] = product.astype(jnp.bfloat16)


def contributions(src_ids, tgt_ids, counts, src_vel, angle, mirror, weights, peers):
    components, rows, cells = src_vel.shape
    slots = weights.shape[0]
    blocks = cells // BLK
    height = components * rows
    peer_rows = slots // peers * height + ID_ROWS
    return pl.pallas_call(
        contribution_kernel,
        out_shape=jax.ShapeDtypeStruct((peers, peer_rows, BLK), jnp.bfloat16),
        in_specs=[
            pl.BlockSpec(memory_space=pltpu.SMEM),
            pl.BlockSpec(memory_space=pltpu.SMEM),
            pl.BlockSpec(memory_space=pltpu.SMEM),
            pl.BlockSpec(memory_space=pltpu.HBM),
            pl.BlockSpec(memory_space=pltpu.HBM),
            pl.BlockSpec(memory_space=pltpu.VMEM),
            pl.BlockSpec(memory_space=pltpu.HBM),
        ],
        out_specs=pl.BlockSpec(memory_space=pltpu.VMEM),
        scratch_shapes=[
            pltpu.VMEM(src_vel.shape, jnp.bfloat16),
            pltpu.VMEM((blocks, BLK), jnp.float32),
            pltpu.VMEM(weights.shape, jnp.bfloat16),
            pltpu.VMEM((blocks, height, BLK), jnp.bfloat16),
            pltpu.SemaphoreType.DMA,
            pltpu.SemaphoreType.DMA,
            pltpu.SemaphoreType.DMA((slots // W_CHUNK,)),
        ],
        compiler_params=pltpu.CompilerParams(vmem_limit_bytes=24 << 20),
        name="contributions",
    )(in_hbm(src_ids), in_hbm(tgt_ids), in_hbm(counts), in_hbm(src_vel), in_hbm(angle.reshape(blocks, BLK)), mirror, in_hbm(weights))


def remap_kernel(recv, eof_ref, out_ref, pcs_ref, eof, acc, ids_vmem, ids_smem, sem):
    components, rows, cells = out_ref.shape
    blocks = cells // BLK
    peers, peer_rows, _ = recv.shape
    height = components * rows
    cap = (peer_rows - ID_ROWS) // height
    for s in range(peers):
        ids = recv[s, cap * height : cap * height + ID_ROWS, :].astype(jnp.float32).astype(jnp.int32)
        ids_vmem[s : s + 1, :] = ids[:1, :]
    copy = pltpu.make_async_copy(ids_vmem, ids_smem, sem)
    copy.start()
    acc[...] = jnp.zeros_like(acc)
    copy.wait()

    def sender(s, carry):
        for j in range(cap):
            start = pl.multiple_of(ids_smem[s, j] * height, height)
            part = recv[s, j * height : (j + 1) * height, :].astype(jnp.float32)
            acc[pl.ds(start, height), :] += part
        return carry

    lax.fori_loop(0, peers, sender, 0)
    for b in range(blocks):
        total = acc[b * height : (b + 1) * height, :].astype(jnp.bfloat16)
        for c in range(components):
            out_ref[c, :, b * BLK : (b + 1) * BLK] = total[c * rows : (c + 1) * rows, :]
    modes = eof_ref.shape[0]
    width = modes // EOF_PARTS
    half = pcs_ref.shape[1]
    pcs_ref[...] = jnp.zeros_like(pcs_ref)
    for i in range(EOF_PARTS):
        eof[i] = jnp.swapaxes(eof_ref[i * width : (i + 1) * width], 0, 1)
        result = 0.0
        for c in range(components):
            result += lax.dot_general(
                out_ref[c], eof[i, c], (((1,), (1,)), ((), ())), preferred_element_type=jnp.float32
            )
        pieces = result.T.reshape(width // (2 * half), 2 * half, rows)
        first = i * width // (2 * half)
        pcs_ref[first : first + width // (2 * half), :, :rows] = pieces[:, :half]
        pcs_ref[first : first + width // (2 * half), :, BLK // 2 : BLK // 2 + rows] = pieces[:, half:]


def remap(received, eofs, rows):
    modes, components, cells = eofs.shape
    peers = received.shape[0]
    height = components * rows
    return pl.pallas_call(
        remap_kernel,
        out_shape=(
            jax.ShapeDtypeStruct((components, rows, cells), jnp.bfloat16),
            jax.ShapeDtypeStruct((peers, modes // peers // 2, BLK), jnp.float32),
        ),
        in_specs=[pl.BlockSpec(memory_space=pltpu.VMEM)] * 2,
        out_specs=(pl.BlockSpec(memory_space=pltpu.VMEM),) * 2,
        scratch_shapes=[
            pltpu.VMEM((EOF_PARTS, components, modes // EOF_PARTS, cells), jnp.bfloat16),
            pltpu.VMEM(((cells // BLK + 1) * height, BLK), jnp.float32),
            pltpu.VMEM((peers, BLK), jnp.int32),
            pltpu.SMEM((peers, BLK), jnp.int32),
            pltpu.SemaphoreType.DMA,
        ],
        compiler_params=pltpu.CompilerParams(vmem_limit_bytes=32 << 20),
        name="remap",
    )(received, eofs)


def per_device(src_vel, angle, src_block, tgt_block, send_count, intersection, eofs):
    components, rows, cells = src_vel.shape
    src_count = lax.axis_size("src")
    tgt_count = lax.axis_size("tgt")
    cap = src_block.shape[3]
    slots = tgt_count * cap
    blocks = eofs.shape[2] // BLK
    edge = src_vel[:, :, cells - BLK :][:, :, ::-1]
    top = (src_count - 1) * tgt_count
    mirror = lax.ppermute(
        edge, ("src", "tgt"), [(top + t, top + tgt_count - 1 - t) for t in range(tgt_count)]
    )
    src_ids = jnp.swapaxes(src_block, 2, 3).reshape(cap, tgt_count)
    tgt_ids = jnp.swapaxes(tgt_block, 2, 3).reshape(cap, tgt_count)
    counts = send_count.reshape(tgt_count)
    weights = intersection.reshape(slots, BLK, BLK)
    contribs = contributions(
        src_ids, tgt_ids, counts, src_vel, angle, mirror, weights, tgt_count
    )
    contribs, eofs = lax.optimization_barrier((contribs, eofs))
    received = lax.all_to_all(contribs, "tgt", split_axis=0, concat_axis=0, tiled=True)
    remapped, partial = remap(received, eofs, rows)
    column = jnp.sum(lax.all_to_all(partial, "tgt", 0, 0, tiled=True), axis=0)
    everyone = jnp.broadcast_to(column[None], (src_count, *column.shape))
    total = jnp.sum(lax.all_to_all(everyone, "src", 0, 0, tiled=True), axis=0)
    pcs = jnp.concatenate([total[:, :rows], total[:, BLK // 2 : BLK // 2 + rows]], axis=0).T
    return remapped, pcs


def solution(mesh):
    return jax.shard_map(
        per_device,
        mesh=mesh,
        in_specs=(
            P(None, None, ("src", "tgt")),
            P(("src", "tgt")),
            P("src", "tgt", None, None),
            P("src", "tgt", None, None),
            P("src", "tgt", None),
            P("src", "tgt", None, None, None, None),
            P(None, None, ("src", "tgt")),
        ),
        out_specs=(P(None, None, ("src", "tgt")), P(None, "tgt")),
        check_vma=False,
    )
```

```python
import jax
import jax.numpy as jnp
from jax import lax
from jax.experimental import pallas as pl
from jax.experimental.pallas import tpu as pltpu
from jax.sharding import PartitionSpec as P

BLK = 128
ID_ROWS = 16
W_CHUNK = 64
EOF_PARTS = 2


def in_hbm(x):
    return pltpu.with_memory_space_constraint(x, pltpu.HBM)


def contribution_kernel(src_ids, tgt_ids, counts, vel_hbm, angle_hbm, mirror_ref, w_hbm, out, vel, angle, w, rot, vel_sem, angle_sem, w_sem):
    components, rows, cells = vel.shape
    blocks = cells // BLK
    slots = w.shape[0]
    peers, peer_rows, _ = out.shape
    cap = slots // peers
    chunks = slots // W_CHUNK
    height = components * rows

    def w_copy(i):
        part = pl.ds(i * W_CHUNK, W_CHUNK)
        return pltpu.make_async_copy(w_hbm.at[part], w.at[part], w_sem.at[i])

    angle_copy = pltpu.make_async_copy(angle_hbm, angle, angle_sem)
    angle_copy.start()
    vel_copy = pltpu.make_async_copy(vel_hbm, vel, vel_sem)
    vel_copy.start()
    for i in range(chunks):
        w_copy(i).start()
    lane = lax.broadcasted_iota(jnp.int32, (ID_ROWS, BLK), 1)
    for d in range(peers):
        ids = jnp.full((ID_ROWS, BLK), blocks, jnp.int32)
        for j in range(cap):
            ids = jnp.where(lane == j, jnp.where(j < counts[d], tgt_ids[j, d], blocks), ids)
        out[d, cap * height :, :] = ids.astype(jnp.float32).astype(jnp.bfloat16)
    top = lax.axis_index("src") == lax.axis_size("src") - 1
    own_share = jnp.where(top, 0.5, 1.0).astype(jnp.float32)
    mirror_share = jnp.where(top, 0.5, 0.0).astype(jnp.float32)
    angle_copy.wait()
    cosine = jnp.cos(angle[...])
    sine = jnp.sin(angle[...])
    vel_copy.wait()
    for b in range(blocks):
        x = vel[0, :, b * BLK : (b + 1) * BLK].astype(jnp.float32)
        y = vel[1, :, b * BLK : (b + 1) * BLK].astype(jnp.float32)
        if b == blocks - 1:
            x = own_share * x - mirror_share * mirror_ref[0].astype(jnp.float32)
            y = own_share * y - mirror_share * mirror_ref[1].astype(jnp.float32)
        c = cosine[b : b + 1, :]
        s = sine[b : b + 1, :]
        rot[b, :rows, :] = (c * x - s * y).astype(jnp.bfloat16)
        rot[b, rows:, :] = (s * x + c * y).astype(jnp.bfloat16)

    for d in range(peers):
        if d * cap % W_CHUNK == 0:
            w_copy(d * cap // W_CHUNK).wait()
        for j in range(cap):
            p = d * cap + j
            block = rot[src_ids[j, d]]
            product = jnp.dot(block, w[p], preferred_element_type=jnp.float32)
            out[d, j * height : (j + 1) * height, :] = product.astype(jnp.bfloat16)


def contributions(src_ids, tgt_ids, counts, src_vel, angle, mirror, weights, peers):
    components, rows, cells = src_vel.shape
    slots = weights.shape[0]
    blocks = cells // BLK
    height = components * rows
    peer_rows = slots // peers * height + ID_ROWS
    return pl.pallas_call(
        contribution_kernel,
        out_shape=jax.ShapeDtypeStruct((peers, peer_rows, BLK), jnp.bfloat16),
        in_specs=[
            pl.BlockSpec(memory_space=pltpu.SMEM),
            pl.BlockSpec(memory_space=pltpu.SMEM),
            pl.BlockSpec(memory_space=pltpu.SMEM),
            pl.BlockSpec(memory_space=pltpu.HBM),
            pl.BlockSpec(memory_space=pltpu.HBM),
            pl.BlockSpec(memory_space=pltpu.VMEM),
            pl.BlockSpec(memory_space=pltpu.HBM),
        ],
        out_specs=pl.BlockSpec(memory_space=pltpu.VMEM),
        scratch_shapes=[
            pltpu.VMEM(src_vel.shape, jnp.bfloat16),
            pltpu.VMEM((blocks, BLK), jnp.float32),
            pltpu.VMEM(weights.shape, jnp.bfloat16),
            pltpu.VMEM((blocks, height, BLK), jnp.bfloat16),
            pltpu.SemaphoreType.DMA,
            pltpu.SemaphoreType.DMA,
            pltpu.SemaphoreType.DMA((slots // W_CHUNK,)),
        ],
        compiler_params=pltpu.CompilerParams(vmem_limit_bytes=24 << 20),
        name="contributions",
    )(in_hbm(src_ids), in_hbm(tgt_ids), in_hbm(counts), in_hbm(src_vel), in_hbm(angle.reshape(blocks, BLK)), mirror, in_hbm(weights))


def remap_kernel(recv, eof_ref, out_ref, pcs_ref, eof, mixed, acc, ids_vmem, ids_smem, sem):
    components, rows, cells = out_ref.shape
    blocks = cells // BLK
    peers, peer_rows, _ = recv.shape
    height = components * rows
    cap = (peer_rows - ID_ROWS) // height
    for s in range(peers):
        ids = recv[s, cap * height : cap * height + ID_ROWS, :].astype(jnp.float32).astype(jnp.int32)
        ids_vmem[s : s + 1, :] = ids[:1, :]
    copy = pltpu.make_async_copy(ids_vmem, ids_smem, sem)
    copy.start()
    modes = eof_ref.shape[0]
    width = modes // EOF_PARTS
    acc[...] = jnp.zeros_like(acc)
    for i in range(EOF_PARTS):
        eof[i] = eof_ref[i * width : (i + 1) * width].reshape(components * width, cells)
    copy.wait()

    def sender(s, carry):
        for j in range(cap):
            start = pl.multiple_of(ids_smem[s, j] * height, height)
            part = recv[s, j * height : (j + 1) * height, :].astype(jnp.float32)
            acc[pl.ds(start, height), :] += part
        return carry

    lax.fori_loop(0, peers, sender, 0)
    for b in range(blocks):
        total = acc[b * height : (b + 1) * height, :].astype(jnp.bfloat16)
        for c in range(components):
            out_ref[c, :, b * BLK : (b + 1) * BLK] = total[c * rows : (c + 1) * rows, :]
    modes = eof_ref.shape[0]
    width = modes // EOF_PARTS
    half = pcs_ref.shape[1]
    pcs_ref[...] = jnp.zeros_like(pcs_ref)
    for i in range(EOF_PARTS):
        product = lax.dot_general(
            out_ref[...].reshape(height, cells),
            eof[i],
            (((1,), (1,)), ((), ())),
            preferred_element_type=jnp.float32,
        )
        mixed[:, :height] = product.T
        result = 0.0
        for c in range(components):
            result += mixed[pl.ds(c, width, stride=components), :][:, c * rows : (c + 1) * rows]
        pieces = result.reshape(width // (2 * half), 2 * half, rows)
        first = i * width // (2 * half)
        pcs_ref[first : first + width // (2 * half), :, :rows] = pieces[:, :half]
        pcs_ref[first : first + width // (2 * half), :, BLK // 2 : BLK // 2 + rows] = pieces[:, half:]


def remap(received, eofs, rows):
    modes, components, cells = eofs.shape
    peers = received.shape[0]
    height = components * rows
    return pl.pallas_call(
        remap_kernel,
        out_shape=(
            jax.ShapeDtypeStruct((components, rows, cells), jnp.bfloat16),
            jax.ShapeDtypeStruct((peers, modes // peers // 2, BLK), jnp.float32),
        ),
        in_specs=[pl.BlockSpec(memory_space=pltpu.VMEM)] * 2,
        out_specs=(pl.BlockSpec(memory_space=pltpu.VMEM),) * 2,
        scratch_shapes=[
            pltpu.VMEM((EOF_PARTS, components * modes // EOF_PARTS, cells), jnp.bfloat16),
            pltpu.VMEM((components * modes // EOF_PARTS, BLK), jnp.float32),
            pltpu.VMEM(((cells // BLK + 1) * height, BLK), jnp.float32),
            pltpu.VMEM((peers, BLK), jnp.int32),
            pltpu.SMEM((peers, BLK), jnp.int32),
            pltpu.SemaphoreType.DMA,
        ],
        compiler_params=pltpu.CompilerParams(vmem_limit_bytes=32 << 20),
        name="remap",
    )(received, eofs)


def per_device(src_vel, angle, src_block, tgt_block, send_count, intersection, eofs):
    components, rows, cells = src_vel.shape
    src_count = lax.axis_size("src")
    tgt_count = lax.axis_size("tgt")
    cap = src_block.shape[3]
    slots = tgt_count * cap
    blocks = eofs.shape[2] // BLK
    edge = src_vel[:, :, cells - BLK :][:, :, ::-1]
    top = (src_count - 1) * tgt_count
    mirror = lax.ppermute(
        edge, ("src", "tgt"), [(top + t, top + tgt_count - 1 - t) for t in range(tgt_count)]
    )
    src_ids = jnp.swapaxes(src_block, 2, 3).reshape(cap, tgt_count)
    tgt_ids = jnp.swapaxes(tgt_block, 2, 3).reshape(cap, tgt_count)
    counts = send_count.reshape(tgt_count)
    weights = intersection.reshape(slots, BLK, BLK)
    contribs = contributions(
        src_ids, tgt_ids, counts, src_vel, angle, mirror, weights, tgt_count
    )
    contribs, eofs = lax.optimization_barrier((contribs, eofs))
    received = lax.all_to_all(contribs, "tgt", split_axis=0, concat_axis=0, tiled=True)
    remapped, partial = remap(received, eofs, rows)
    column = jnp.sum(lax.all_to_all(partial, "tgt", 0, 0, tiled=True), axis=0)
    everyone = jnp.broadcast_to(column[None], (src_count, *column.shape))
    total = jnp.sum(lax.all_to_all(everyone, "src", 0, 0, tiled=True), axis=0)
    pcs = jnp.concatenate([total[:, :rows], total[:, BLK // 2 : BLK // 2 + rows]], axis=0).T
    return remapped, pcs


def solution(mesh):
    return jax.shard_map(
        per_device,
        mesh=mesh,
        in_specs=(
            P(None, None, ("src", "tgt")),
            P(("src", "tgt")),
            P("src", "tgt", None, None),
            P("src", "tgt", None, None),
            P("src", "tgt", None),
            P("src", "tgt", None, None, None, None),
            P(None, None, ("src", "tgt")),
        ),
        out_specs=(P(None, None, ("src", "tgt")), P(None, "tgt")),
        check_vma=False,
    )
```

```python
import jax
import jax.numpy as jnp
from jax import lax
from jax.experimental import pallas as pl
from jax.experimental.pallas import tpu as pltpu
from jax.sharding import PartitionSpec as P

BLK = 128
ID_ROWS = 8
W_CHUNK = 64
EOF_PARTS = 2


def in_hbm(x):
    return pltpu.with_memory_space_constraint(x, pltpu.HBM)


def contribution_kernel(
    src_ids_hbm,
    tgt_ids_hbm,
    counts_hbm,
    vel_hbm,
    angle_hbm,
    w_hbm,
    out,
    w,
    trig,
    src_ids,
    tgt_ids,
    counts,
    vel,
    angle,
    rot,
    small_sem,
    vel_sem,
    w_sem,
):
    components, rows, cells = vel.shape
    blocks = cells // BLK
    slots = w.shape[0]
    peers, peer_rows, _ = out.shape
    cap = slots // peers
    chunks = slots // W_CHUNK
    height = components * rows

    def w_copy(i):
        part = pl.ds(i * W_CHUNK, W_CHUNK)
        return pltpu.make_async_copy(w_hbm.at[part], w.at[part], w_sem.at[i])

    small = [
        pltpu.make_async_copy(src, dst, small_sem.at[i])
        for i, (src, dst) in enumerate(
            [(src_ids_hbm, src_ids), (tgt_ids_hbm, tgt_ids), (counts_hbm, counts), (angle_hbm, angle)]
        )
    ]
    for copy in small:
        copy.start()
    vel_copy = pltpu.make_async_copy(vel_hbm, vel, vel_sem)
    vel_copy.start()
    for i in range(chunks):
        w_copy(i).start()
    for copy in small:
        copy.wait()
    lane = lax.broadcasted_iota(jnp.int32, (ID_ROWS, BLK), 1)
    for d in range(peers):
        ids = jnp.full((ID_ROWS, BLK), blocks, jnp.int32)
        for j in range(cap):
            ids = jnp.where(lane == j, jnp.where(j < counts[d], tgt_ids[j, d], blocks), ids)
        out[d, cap * height :, :] = ids.astype(jnp.float32).astype(jnp.bfloat16)
    cosine = jnp.cos(angle[...])
    sine = jnp.sin(angle[...])
    trig[0] = cosine
    trig[1] = sine
    vel_copy.wait()
    for b in range(blocks):
        x = vel[0, :, b * BLK : (b + 1) * BLK].astype(jnp.float32)
        y = vel[1, :, b * BLK : (b + 1) * BLK].astype(jnp.float32)
        c = cosine[b : b + 1, :]
        s = sine[b : b + 1, :]
        rot[b, :rows, :] = (c * x - s * y).astype(jnp.bfloat16)
        rot[b, rows:, :] = (s * x + c * y).astype(jnp.bfloat16)

    for d in range(peers):
        if d * cap % W_CHUNK == 0:
            w_copy(d * cap // W_CHUNK).wait()
        for j in range(cap):
            p = d * cap + j
            block = rot[src_ids[j, d]]
            product = jnp.dot(block, w[p], preferred_element_type=jnp.float32)
            out[d, j * height : (j + 1) * height, :] = product.astype(jnp.bfloat16)


def contributions(src_ids, tgt_ids, counts, src_vel, angle, weights, peers):
    components, rows, cells = src_vel.shape
    slots = weights.shape[0]
    blocks = cells // BLK
    height = components * rows
    peer_rows = slots // peers * height + ID_ROWS
    return pl.pallas_call(
        contribution_kernel,
        out_shape=(
            jax.ShapeDtypeStruct((peers, peer_rows, BLK), jnp.bfloat16),
            jax.ShapeDtypeStruct(weights.shape, jnp.bfloat16),
            jax.ShapeDtypeStruct((2, blocks, BLK), jnp.float32),
        ),
        in_specs=[
            pl.BlockSpec(memory_space=pltpu.HBM),
        ]
        * 6,
        out_specs=(pl.BlockSpec(memory_space=pltpu.VMEM),) * 3,
        scratch_shapes=[
            pltpu.SMEM(src_ids.shape, jnp.int32),
            pltpu.SMEM(tgt_ids.shape, jnp.int32),
            pltpu.SMEM(counts.shape, jnp.int32),
            pltpu.VMEM(src_vel.shape, jnp.bfloat16),
            pltpu.VMEM((blocks, BLK), jnp.float32),
            pltpu.VMEM((blocks, height, BLK), jnp.bfloat16),
            pltpu.SemaphoreType.DMA((4,)),
            pltpu.SemaphoreType.DMA,
            pltpu.SemaphoreType.DMA((slots // W_CHUNK,)),
        ],
        compiler_params=pltpu.CompilerParams(vmem_limit_bytes=24 << 20),
        name="contributions",
    )(in_hbm(src_ids), in_hbm(tgt_ids), in_hbm(counts), in_hbm(src_vel), in_hbm(angle.reshape(blocks, BLK)), in_hbm(weights))


def fold_kernel(given, w, trig, edge, mirror, ids_hbm, out, block, ids, sem):
    _, rows, _ = edge.shape
    blocks = trig.shape[1]
    peers = out.shape[0]
    cap = ids.shape[0]
    height = block.shape[0]

    @pl.when(lax.axis_index("src") == lax.axis_size("src") - 1)
    def _():
        copy = pltpu.make_async_copy(ids_hbm, ids, sem)
        copy.start()
        x = 0.5 * (edge[0].astype(jnp.float32) - mirror[0].astype(jnp.float32))
        y = 0.5 * (edge[1].astype(jnp.float32) - mirror[1].astype(jnp.float32))
        c = trig[0, blocks - 1 : blocks, :]
        s = trig[1, blocks - 1 : blocks, :]
        block[:rows, :] = (c * x - s * y).astype(jnp.bfloat16)
        block[rows:, :] = (s * x + c * y).astype(jnp.bfloat16)
        copy.wait()
        for d in range(peers):
            for j in range(cap):

                @pl.when(ids[j, d] == blocks - 1)
                def _():
                    product = jnp.dot(block[...], w[d * cap + j], preferred_element_type=jnp.float32)
                    out[d, j * height : (j + 1) * height, :] = product.astype(jnp.bfloat16)


def fold(contribs, weights, trig, edge, mirror, src_ids):
    components, rows, _ = edge.shape
    return pl.pallas_call(
        fold_kernel,
        out_shape=jax.ShapeDtypeStruct(contribs.shape, contribs.dtype),
        in_specs=[pl.BlockSpec(memory_space=pltpu.VMEM)] * 5 + [pl.BlockSpec(memory_space=pltpu.HBM)],
        out_specs=pl.BlockSpec(memory_space=pltpu.VMEM),
        scratch_shapes=[
            pltpu.VMEM((components * rows, BLK), jnp.bfloat16),
            pltpu.SMEM(src_ids.shape, jnp.int32),
            pltpu.SemaphoreType.DMA,
        ],
        input_output_aliases={0: 0},
        compiler_params=pltpu.CompilerParams(vmem_limit_bytes=16 << 20),
        name="fold",
    )(contribs, weights, trig, edge, mirror, in_hbm(src_ids))


def remap_kernel(recv, eof_ref, out_ref, pcs_ref, eof, mixed, acc, ids_vmem, ids_smem, sem):
    components, rows, cells = out_ref.shape
    blocks = cells // BLK
    peers, peer_rows, _ = recv.shape
    height = components * rows
    cap = (peer_rows - ID_ROWS) // height
    for s in range(peers):
        ids = recv[s, cap * height : cap * height + ID_ROWS, :].astype(jnp.float32).astype(jnp.int32)
        ids_vmem[s : s + 1, :] = ids[:1, :]
    copy = pltpu.make_async_copy(ids_vmem, ids_smem, sem)
    copy.start()
    modes = eof_ref.shape[0]
    width = modes // EOF_PARTS
    acc[...] = jnp.zeros_like(acc)
    for i in range(EOF_PARTS):
        eof[i] = eof_ref[i * width : (i + 1) * width].reshape(components * width, cells)
    copy.wait()

    def sender(s, carry):
        for j in range(cap):
            start = pl.multiple_of(ids_smem[s, j] * height, height)
            part = recv[s, j * height : (j + 1) * height, :].astype(jnp.float32)
            acc[pl.ds(start, height), :] += part
        return carry

    lax.fori_loop(0, peers, sender, 0)
    for b in range(blocks):
        total = acc[b * height : (b + 1) * height, :].astype(jnp.bfloat16)
        for c in range(components):
            out_ref[c, :, b * BLK : (b + 1) * BLK] = total[c * rows : (c + 1) * rows, :]
    modes = eof_ref.shape[0]
    width = modes // EOF_PARTS
    half = pcs_ref.shape[1]
    pcs_ref[...] = jnp.zeros_like(pcs_ref)
    for i in range(EOF_PARTS):
        product = lax.dot_general(
            out_ref[...].reshape(height, cells),
            eof[i],
            (((1,), (1,)), ((), ())),
            preferred_element_type=jnp.float32,
        )
        mixed[:, :height] = product.T
        result = 0.0
        for c in range(components):
            result += mixed[pl.ds(c, width, stride=components), :][:, c * rows : (c + 1) * rows]
        pieces = result.reshape(width // (2 * half), 2 * half, rows)
        first = i * width // (2 * half)
        pcs_ref[first : first + width // (2 * half), :, :rows] = pieces[:, :half]
        pcs_ref[first : first + width // (2 * half), :, BLK // 2 : BLK // 2 + rows] = pieces[:, half:]


def remap(received, eofs, rows):
    modes, components, cells = eofs.shape
    peers = received.shape[0]
    height = components * rows
    return pl.pallas_call(
        remap_kernel,
        out_shape=(
            jax.ShapeDtypeStruct((components, rows, cells), jnp.bfloat16),
            jax.ShapeDtypeStruct((peers, modes // peers // 2, BLK), jnp.float32),
        ),
        in_specs=[pl.BlockSpec(memory_space=pltpu.VMEM)] * 2,
        out_specs=(pl.BlockSpec(memory_space=pltpu.VMEM),) * 2,
        scratch_shapes=[
            pltpu.VMEM((EOF_PARTS, components * modes // EOF_PARTS, cells), jnp.bfloat16),
            pltpu.VMEM((components * modes // EOF_PARTS, BLK), jnp.float32),
            pltpu.VMEM(((cells // BLK + 1) * height, BLK), jnp.float32),
            pltpu.VMEM((peers, BLK), jnp.int32),
            pltpu.SMEM((peers, BLK), jnp.int32),
            pltpu.SemaphoreType.DMA,
        ],
        compiler_params=pltpu.CompilerParams(vmem_limit_bytes=32 << 20),
        name="remap",
    )(received, eofs)


def per_device(src_vel, angle, src_block, tgt_block, send_count, intersection, eofs):
    components, rows, cells = src_vel.shape
    src_count = lax.axis_size("src")
    tgt_count = lax.axis_size("tgt")
    cap = src_block.shape[3]
    slots = tgt_count * cap
    blocks = eofs.shape[2] // BLK
    edge = src_vel[:, :, cells - BLK :]
    top = (src_count - 1) * tgt_count
    mirror = lax.ppermute(
        edge[:, :, ::-1], ("src", "tgt"), [(top + t, top + tgt_count - 1 - t) for t in range(tgt_count)]
    )
    src_ids = jnp.swapaxes(src_block, 2, 3).reshape(cap, tgt_count)
    tgt_ids = jnp.swapaxes(tgt_block, 2, 3).reshape(cap, tgt_count)
    counts = send_count.reshape(tgt_count)
    weights = intersection.reshape(slots, BLK, BLK)
    contribs, weights, trig = contributions(
        src_ids, tgt_ids, counts, src_vel, angle, weights, tgt_count
    )
    contribs = fold(contribs, weights, trig, edge, mirror, src_ids)
    received = lax.all_to_all(contribs, "tgt", split_axis=0, concat_axis=0, tiled=True)
    remapped, partial = remap(received, eofs, rows)
    column = jnp.sum(lax.all_to_all(partial, "tgt", 0, 0, tiled=True), axis=0)
    everyone = jnp.broadcast_to(column[None], (src_count, *column.shape))
    total = jnp.sum(lax.all_to_all(everyone, "src", 0, 0, tiled=True), axis=0)
    pcs = jnp.concatenate([total[:, :rows], total[:, BLK // 2 : BLK // 2 + rows]], axis=0).T
    return remapped, pcs


def solution(mesh):
    return jax.shard_map(
        per_device,
        mesh=mesh,
        in_specs=(
            P(None, None, ("src", "tgt")),
            P(("src", "tgt")),
            P("src", "tgt", None, None),
            P("src", "tgt", None, None),
            P("src", "tgt", None),
            P("src", "tgt", None, None, None, None),
            P(None, None, ("src", "tgt")),
        ),
        out_specs=(P(None, None, ("src", "tgt")), P(None, "tgt")),
        check_vma=False,
    )
```

```python
import jax
import jax.numpy as jnp
from jax import lax
from jax.experimental import pallas as pl
from jax.experimental.pallas import tpu as pltpu
from jax.sharding import PartitionSpec as P

BLK = 128
ID_ROWS = 8
W_CHUNK = 64
EOF_PARTS = 2


def in_hbm(x):
    return pltpu.with_memory_space_constraint(x, pltpu.HBM)


def contribution_kernel(
    src_ids_hbm,
    tgt_ids_hbm,
    counts_hbm,
    vel_hbm,
    angle_hbm,
    w_hbm,
    out,
    w,
    trig,
    src_ids,
    tgt_ids,
    counts,
    vel,
    angle,
    rot,
    small_sem,
    vel_sem,
    w_sem,
):
    components, rows, cells = vel.shape
    blocks = cells // BLK
    slots = w.shape[0]
    peers, peer_rows, _ = out.shape
    cap = slots // peers
    chunks = slots // W_CHUNK
    height = components * rows

    def w_copy(i):
        part = pl.ds(i * W_CHUNK, W_CHUNK)
        return pltpu.make_async_copy(w_hbm.at[part], w.at[part], w_sem.at[i])

    small = [
        pltpu.make_async_copy(src, dst, small_sem.at[i])
        for i, (src, dst) in enumerate(
            [(src_ids_hbm, src_ids), (tgt_ids_hbm, tgt_ids), (counts_hbm, counts), (angle_hbm, angle)]
        )
    ]
    for copy in small:
        copy.start()
    vel_copy = pltpu.make_async_copy(vel_hbm, vel, vel_sem)
    vel_copy.start()
    for i in range(chunks):
        w_copy(i).start()
    for copy in small:
        copy.wait()
    lane = lax.broadcasted_iota(jnp.int32, (ID_ROWS, BLK), 1)
    for d in range(peers):
        ids = jnp.full((ID_ROWS, BLK), blocks, jnp.int32)
        for j in range(cap):
            ids = jnp.where(lane == j, jnp.where(j < counts[d], tgt_ids[j, d], blocks), ids)
        out[d, cap * height :, :] = ids.astype(jnp.float32).astype(jnp.bfloat16)
    cosine = jnp.cos(angle[...])
    sine = jnp.sin(angle[...])
    trig[0] = cosine
    trig[1] = sine
    vel_copy.wait()
    for b in range(blocks):
        x = vel[0, :, b * BLK : (b + 1) * BLK].astype(jnp.float32)
        y = vel[1, :, b * BLK : (b + 1) * BLK].astype(jnp.float32)
        c = cosine[b : b + 1, :]
        s = sine[b : b + 1, :]
        rot[b, :rows, :] = (c * x - s * y).astype(jnp.bfloat16)
        rot[b, rows:, :] = (s * x + c * y).astype(jnp.bfloat16)

    for d in range(peers):
        if d * cap % W_CHUNK == 0:
            w_copy(d * cap // W_CHUNK).wait()
        for j in range(cap):
            p = d * cap + j
            block = rot[src_ids[j, d]]
            product = jnp.dot(block, w[p], preferred_element_type=jnp.float32)
            out[d, j * height : (j + 1) * height, :] = product.astype(jnp.bfloat16)


def contributions(src_ids, tgt_ids, counts, src_vel, angle, weights, peers):
    components, rows, cells = src_vel.shape
    slots = weights.shape[0]
    blocks = cells // BLK
    height = components * rows
    peer_rows = slots // peers * height + ID_ROWS
    return pl.pallas_call(
        contribution_kernel,
        out_shape=(
            jax.ShapeDtypeStruct((peers, peer_rows, BLK), jnp.bfloat16),
            jax.ShapeDtypeStruct(weights.shape, jnp.bfloat16),
            jax.ShapeDtypeStruct((2, blocks, BLK), jnp.float32),
        ),
        in_specs=[
            pl.BlockSpec(memory_space=pltpu.HBM),
        ]
        * 6,
        out_specs=(pl.BlockSpec(memory_space=pltpu.VMEM),) * 3,
        scratch_shapes=[
            pltpu.SMEM(src_ids.shape, jnp.int32),
            pltpu.SMEM(tgt_ids.shape, jnp.int32),
            pltpu.SMEM(counts.shape, jnp.int32),
            pltpu.VMEM(src_vel.shape, jnp.bfloat16),
            pltpu.VMEM((blocks, BLK), jnp.float32),
            pltpu.VMEM((blocks, height, BLK), jnp.bfloat16),
            pltpu.SemaphoreType.DMA((4,)),
            pltpu.SemaphoreType.DMA,
            pltpu.SemaphoreType.DMA((slots // W_CHUNK,)),
        ],
        compiler_params=pltpu.CompilerParams(vmem_limit_bytes=24 << 20),
        name="contributions",
    )(in_hbm(src_ids), in_hbm(tgt_ids), in_hbm(counts), in_hbm(src_vel), in_hbm(angle.reshape(blocks, BLK)), in_hbm(weights))


def fold_kernel(given, w, trig, edge, mirror, ids_hbm, out, block, ids, sem):
    _, rows, _ = edge.shape
    blocks = trig.shape[1]
    peers = out.shape[0]
    cap = ids.shape[0]
    height = block.shape[0]

    @pl.when(lax.axis_index("src") == lax.axis_size("src") - 1)
    def _():
        copy = pltpu.make_async_copy(ids_hbm, ids, sem)
        copy.start()
        x = 0.5 * (edge[0].astype(jnp.float32) - mirror[0].astype(jnp.float32))
        y = 0.5 * (edge[1].astype(jnp.float32) - mirror[1].astype(jnp.float32))
        c = trig[0, blocks - 1 : blocks, :]
        s = trig[1, blocks - 1 : blocks, :]
        block[:rows, :] = (c * x - s * y).astype(jnp.bfloat16)
        block[rows:, :] = (s * x + c * y).astype(jnp.bfloat16)
        copy.wait()
        for d in range(peers):
            for j in range(cap):

                @pl.when(ids[j, d] == blocks - 1)
                def _():
                    product = jnp.dot(block[...], w[d * cap + j], preferred_element_type=jnp.float32)
                    out[d, j * height : (j + 1) * height, :] = product.astype(jnp.bfloat16)


def fold(contribs, weights, trig, edge, mirror, src_ids):
    components, rows, _ = edge.shape
    return pl.pallas_call(
        fold_kernel,
        out_shape=jax.ShapeDtypeStruct(contribs.shape, contribs.dtype),
        in_specs=[pl.BlockSpec(memory_space=pltpu.VMEM)] * 5 + [pl.BlockSpec(memory_space=pltpu.HBM)],
        out_specs=pl.BlockSpec(memory_space=pltpu.VMEM),
        scratch_shapes=[
            pltpu.VMEM((components * rows, BLK), jnp.bfloat16),
            pltpu.SMEM(src_ids.shape, jnp.int32),
            pltpu.SemaphoreType.DMA,
        ],
        input_output_aliases={0: 0},
        compiler_params=pltpu.CompilerParams(vmem_limit_bytes=16 << 20),
        name="fold",
    )(contribs, weights, trig, edge, mirror, in_hbm(src_ids))


def remap_kernel(recv, eof_ref, out_ref, pcs_ref, eof, mixed, acc, ids_vmem, ids_smem, sem):
    components, rows, cells = out_ref.shape
    blocks = cells // BLK
    peers, peer_rows, _ = recv.shape
    height = components * rows
    cap = (peer_rows - ID_ROWS) // height
    for s in range(peers):
        ids = recv[s, cap * height : cap * height + ID_ROWS, :].astype(jnp.float32).astype(jnp.int32)
        ids_vmem[s : s + 1, :] = ids[:1, :]
    copy = pltpu.make_async_copy(ids_vmem, ids_smem, sem)
    copy.start()
    modes = eof_ref.shape[0]
    width = modes // EOF_PARTS
    acc[...] = jnp.zeros_like(acc)
    for i in range(EOF_PARTS):
        eof[i] = eof_ref[i * width : (i + 1) * width].reshape(components * width, cells)
    copy.wait()

    def sender(s, carry):
        for j in range(cap):
            start = pl.multiple_of(ids_smem[s, j] * height, height)
            part = recv[s, j * height : (j + 1) * height, :].astype(jnp.float32)
            acc[pl.ds(start, height), :] += part
        return carry

    lax.fori_loop(0, peers, sender, 0)
    for b in range(blocks):
        total = acc[b * height : (b + 1) * height, :].astype(jnp.bfloat16)
        for c in range(components):
            out_ref[c, :, b * BLK : (b + 1) * BLK] = total[c * rows : (c + 1) * rows, :]
    modes = eof_ref.shape[0]
    width = modes // EOF_PARTS
    half = pcs_ref.shape[1]
    pcs_ref[...] = jnp.zeros_like(pcs_ref)
    for i in range(EOF_PARTS):
        product = lax.dot_general(
            out_ref[...].reshape(height, cells),
            eof[i],
            (((1,), (1,)), ((), ())),
            preferred_element_type=jnp.float32,
        )
        mixed[:, :height] = product.T
        result = 0.0
        for c in range(components):
            result += mixed[pl.ds(c, width, stride=components), :][:, c * rows : (c + 1) * rows]
        pieces = result.reshape(width // (2 * half), 2 * half, rows)
        first = i * width // (2 * half)
        pcs_ref[first : first + width // (2 * half), :, :rows] = pieces[:, :half]
        pcs_ref[first : first + width // (2 * half), :, BLK // 2 : BLK // 2 + rows] = pieces[:, half:]


def remap(received, eofs, rows):
    modes, components, cells = eofs.shape
    peers = received.shape[0]
    height = components * rows
    return pl.pallas_call(
        remap_kernel,
        out_shape=(
            jax.ShapeDtypeStruct((components, rows, cells), jnp.bfloat16),
            jax.ShapeDtypeStruct((peers, modes // peers // 2, BLK), jnp.float32),
        ),
        in_specs=[pl.BlockSpec(memory_space=pltpu.VMEM)] * 2,
        out_specs=(pl.BlockSpec(memory_space=pltpu.VMEM),) * 2,
        scratch_shapes=[
            pltpu.VMEM((EOF_PARTS, components * modes // EOF_PARTS, cells), jnp.bfloat16),
            pltpu.VMEM((components * modes // EOF_PARTS, BLK), jnp.float32),
            pltpu.VMEM(((cells // BLK + 1) * height, BLK), jnp.float32),
            pltpu.VMEM((peers, BLK), jnp.int32),
            pltpu.SMEM((peers, BLK), jnp.int32),
            pltpu.SemaphoreType.DMA,
        ],
        compiler_params=pltpu.CompilerParams(vmem_limit_bytes=32 << 20),
        name="remap",
    )(received, eofs)


def from_row(x, to):
    return lax.ppermute(x, "src", [(row, to(row)) for row in range(lax.axis_size("src"))])


def per_device(src_vel, angle, src_block, tgt_block, send_count, intersection, eofs):
    components, rows, cells = src_vel.shape
    src_count = lax.axis_size("src")
    tgt_count = lax.axis_size("tgt")
    cap = src_block.shape[3]
    slots = tgt_count * cap
    blocks = eofs.shape[2] // BLK
    edge = src_vel[:, :, cells - BLK :]
    top = (src_count - 1) * tgt_count
    mirror = lax.ppermute(
        edge[:, :, ::-1], ("src", "tgt"), [(top + t, top + tgt_count - 1 - t) for t in range(tgt_count)]
    )
    src_ids = jnp.swapaxes(src_block, 2, 3).reshape(cap, tgt_count)
    tgt_ids = jnp.swapaxes(tgt_block, 2, 3).reshape(cap, tgt_count)
    counts = send_count.reshape(tgt_count)
    weights = intersection.reshape(slots, BLK, BLK)
    contribs, weights, trig = contributions(
        src_ids, tgt_ids, counts, src_vel, angle, weights, tgt_count
    )
    contribs = fold(contribs, weights, trig, edge, mirror, src_ids)
    received = lax.all_to_all(contribs, "tgt", split_axis=0, concat_axis=0, tiled=True)
    remapped, partial = remap(received, eofs, rows)
    column = jnp.sum(lax.all_to_all(partial, "tgt", 0, 0, tiled=True), axis=0)
    pair = column + from_row(column, lambda row: row ^ 1)
    one, two, three = (
        from_row(pair, lambda row, k=k: (row + 2 * k) % src_count) for k in range(1, src_count // 2)
    )
    total = (pair + two) + (one + three)
    pcs = jnp.concatenate([total[:, :rows], total[:, BLK // 2 : BLK // 2 + rows]], axis=0).T
    return remapped, pcs


def solution(mesh):
    return jax.shard_map(
        per_device,
        mesh=mesh,
        in_specs=(
            P(None, None, ("src", "tgt")),
            P(("src", "tgt")),
            P("src", "tgt", None, None),
            P("src", "tgt", None, None),
            P("src", "tgt", None),
            P("src", "tgt", None, None, None, None),
            P(None, None, ("src", "tgt")),
        ),
        out_specs=(P(None, None, ("src", "tgt")), P(None, "tgt")),
        check_vma=False,
    )
```

```python
import jax
import jax.numpy as jnp
from jax import lax
from jax.experimental import pallas as pl
from jax.experimental.pallas import tpu as pltpu
from jax.sharding import PartitionSpec as P

BLK = 128
ID_ROWS = 8
W_CHUNK = 64
EOF_PARTS = 1


def in_hbm(x):
    return pltpu.with_memory_space_constraint(x, pltpu.HBM)


def contribution_kernel(
    src_ids_hbm,
    tgt_ids_hbm,
    counts_hbm,
    vel_hbm,
    angle_hbm,
    w_hbm,
    out,
    w,
    trig,
    src_ids,
    tgt_ids,
    counts,
    vel,
    angle,
    rot,
    small_sem,
    vel_sem,
    w_sem,
):
    components, rows, cells = vel.shape
    blocks = cells // BLK
    slots = w.shape[0]
    peers, peer_rows, _ = out.shape
    cap = slots // peers
    chunks = slots // W_CHUNK
    height = components * rows

    def w_copy(i):
        part = pl.ds(i * W_CHUNK, W_CHUNK)
        return pltpu.make_async_copy(w_hbm.at[part], w.at[part], w_sem.at[i])

    small = [
        pltpu.make_async_copy(src, dst, small_sem.at[i])
        for i, (src, dst) in enumerate(
            [(src_ids_hbm, src_ids), (tgt_ids_hbm, tgt_ids), (counts_hbm, counts), (angle_hbm, angle)]
        )
    ]
    for copy in small:
        copy.start()
    vel_copy = pltpu.make_async_copy(vel_hbm, vel, vel_sem)
    vel_copy.start()
    for i in range(chunks):
        w_copy(i).start()
    for copy in small:
        copy.wait()
    lane = lax.broadcasted_iota(jnp.int32, (ID_ROWS, BLK), 1)
    for d in range(peers):
        ids = jnp.full((ID_ROWS, BLK), blocks, jnp.int32)
        for j in range(cap):
            ids = jnp.where(lane == j, jnp.where(j < counts[d], tgt_ids[j, d], blocks), ids)
        out[d, cap * height :, :] = ids.astype(jnp.float32).astype(jnp.bfloat16)
    cosine = jnp.cos(angle[...])
    sine = jnp.sin(angle[...])
    trig[0] = cosine
    trig[1] = sine
    vel_copy.wait()
    for b in range(blocks):
        x = vel[0, :, b * BLK : (b + 1) * BLK].astype(jnp.float32)
        y = vel[1, :, b * BLK : (b + 1) * BLK].astype(jnp.float32)
        c = cosine[b : b + 1, :]
        s = sine[b : b + 1, :]
        rot[b, :rows, :] = (c * x - s * y).astype(jnp.bfloat16)
        rot[b, rows:, :] = (s * x + c * y).astype(jnp.bfloat16)

    for d in range(peers):
        if d * cap % W_CHUNK == 0:
            w_copy(d * cap // W_CHUNK).wait()
        for j in range(cap):
            p = d * cap + j
            block = rot[src_ids[j, d]]
            product = jnp.dot(block, w[p], preferred_element_type=jnp.float32)
            out[d, j * height : (j + 1) * height, :] = product.astype(jnp.bfloat16)


def contributions(src_ids, tgt_ids, counts, src_vel, angle, weights, peers):
    components, rows, cells = src_vel.shape
    slots = weights.shape[0]
    blocks = cells // BLK
    height = components * rows
    peer_rows = slots // peers * height + ID_ROWS
    return pl.pallas_call(
        contribution_kernel,
        out_shape=(
            jax.ShapeDtypeStruct((peers, peer_rows, BLK), jnp.bfloat16),
            jax.ShapeDtypeStruct(weights.shape, jnp.bfloat16),
            jax.ShapeDtypeStruct((2, blocks, BLK), jnp.float32),
        ),
        in_specs=[
            pl.BlockSpec(memory_space=pltpu.HBM),
        ]
        * 6,
        out_specs=(pl.BlockSpec(memory_space=pltpu.VMEM),) * 3,
        scratch_shapes=[
            pltpu.SMEM(src_ids.shape, jnp.int32),
            pltpu.SMEM(tgt_ids.shape, jnp.int32),
            pltpu.SMEM(counts.shape, jnp.int32),
            pltpu.VMEM(src_vel.shape, jnp.bfloat16),
            pltpu.VMEM((blocks, BLK), jnp.float32),
            pltpu.VMEM((blocks, height, BLK), jnp.bfloat16),
            pltpu.SemaphoreType.DMA((4,)),
            pltpu.SemaphoreType.DMA,
            pltpu.SemaphoreType.DMA((slots // W_CHUNK,)),
        ],
        compiler_params=pltpu.CompilerParams(vmem_limit_bytes=24 << 20),
        name="contributions",
    )(in_hbm(src_ids), in_hbm(tgt_ids), in_hbm(counts), in_hbm(src_vel), in_hbm(angle.reshape(blocks, BLK)), in_hbm(weights))


def fold_kernel(given, w, trig, edge, mirror, ids_hbm, out, block, ids, sem):
    _, rows, _ = edge.shape
    blocks = trig.shape[1]
    peers = out.shape[0]
    cap = ids.shape[0]
    height = block.shape[0]

    @pl.when(lax.axis_index("src") == lax.axis_size("src") - 1)
    def _():
        copy = pltpu.make_async_copy(ids_hbm, ids, sem)
        copy.start()
        lane = lax.broadcasted_iota(jnp.int32, (BLK, BLK), 0)
        flip = (lane + lax.broadcasted_iota(jnp.int32, (BLK, BLK), 1) == BLK - 1).astype(jnp.float32)
        flip = flip.astype(jnp.bfloat16)
        x, y = (
            0.5 * (edge[c].astype(jnp.float32) - jnp.dot(mirror[c], flip, preferred_element_type=jnp.float32))
            for c in range(2)
        )
        c = trig[0, blocks - 1 : blocks, :]
        s = trig[1, blocks - 1 : blocks, :]
        block[:rows, :] = (c * x - s * y).astype(jnp.bfloat16)
        block[rows:, :] = (s * x + c * y).astype(jnp.bfloat16)
        copy.wait()
        for d in range(peers):
            for j in range(cap):

                @pl.when(ids[j, d] == blocks - 1)
                def _():
                    product = jnp.dot(block[...], w[d * cap + j], preferred_element_type=jnp.float32)
                    out[d, j * height : (j + 1) * height, :] = product.astype(jnp.bfloat16)


def fold(contribs, weights, trig, edge, mirror, src_ids):
    components, rows, _ = edge.shape
    return pl.pallas_call(
        fold_kernel,
        out_shape=jax.ShapeDtypeStruct(contribs.shape, contribs.dtype),
        in_specs=[pl.BlockSpec(memory_space=pltpu.VMEM)] * 5 + [pl.BlockSpec(memory_space=pltpu.HBM)],
        out_specs=pl.BlockSpec(memory_space=pltpu.VMEM),
        scratch_shapes=[
            pltpu.VMEM((components * rows, BLK), jnp.bfloat16),
            pltpu.SMEM(src_ids.shape, jnp.int32),
            pltpu.SemaphoreType.DMA,
        ],
        input_output_aliases={0: 0},
        compiler_params=pltpu.CompilerParams(vmem_limit_bytes=16 << 20),
        name="fold",
    )(contribs, weights, trig, edge, mirror, in_hbm(src_ids))


def remap_kernel(recv, eof_ref, out_ref, pcs_ref, eof, mixed, acc, ids_vmem, ids_smem, sem):
    components, rows, cells = out_ref.shape
    blocks = cells // BLK
    peers, peer_rows, _ = recv.shape
    height = components * rows
    cap = (peer_rows - ID_ROWS) // height
    for s in range(peers):
        ids = recv[s, cap * height : cap * height + ID_ROWS, :].astype(jnp.float32).astype(jnp.int32)
        ids_vmem[s : s + 1, :] = ids[:1, :]
    copy = pltpu.make_async_copy(ids_vmem, ids_smem, sem)
    copy.start()
    modes = eof_ref.shape[0]
    width = modes // EOF_PARTS
    acc[...] = jnp.zeros_like(acc)
    for i in range(EOF_PARTS):
        eof[i] = eof_ref[i * width : (i + 1) * width].reshape(components * width, cells)
    copy.wait()

    def sender(s, carry):
        for j in range(cap):
            start = pl.multiple_of(ids_smem[s, j] * height, height)
            part = recv[s, j * height : (j + 1) * height, :].astype(jnp.float32)
            acc[pl.ds(start, height), :] += part
        return carry

    lax.fori_loop(0, peers, sender, 0, unroll=2)
    for b in range(blocks):
        total = acc[b * height : (b + 1) * height, :].astype(jnp.bfloat16)
        for c in range(components):
            out_ref[c, :, b * BLK : (b + 1) * BLK] = total[c * rows : (c + 1) * rows, :]
    modes = eof_ref.shape[0]
    width = modes // EOF_PARTS
    half = pcs_ref.shape[1]
    pcs_ref[...] = jnp.zeros_like(pcs_ref)
    for i in range(EOF_PARTS):
        product = lax.dot_general(
            out_ref[...].reshape(height, cells),
            eof[i],
            (((1,), (1,)), ((), ())),
            preferred_element_type=jnp.float32,
        )
        mixed[:, :height] = product.T
        result = 0.0
        for c in range(components):
            result += mixed[pl.ds(c, width, stride=components), :][:, c * rows : (c + 1) * rows]
        pieces = result.reshape(width // (2 * half), 2 * half, rows)
        first = i * width // (2 * half)
        pcs_ref[first : first + width // (2 * half), :, :rows] = pieces[:, :half]
        pcs_ref[first : first + width // (2 * half), :, BLK // 2 : BLK // 2 + rows] = pieces[:, half:]


def remap(received, eofs, rows):
    modes, components, cells = eofs.shape
    peers = received.shape[0]
    height = components * rows
    return pl.pallas_call(
        remap_kernel,
        out_shape=(
            jax.ShapeDtypeStruct((components, rows, cells), jnp.bfloat16),
            jax.ShapeDtypeStruct((peers, modes // peers // 2, BLK), jnp.float32),
        ),
        in_specs=[pl.BlockSpec(memory_space=pltpu.VMEM)] * 2,
        out_specs=(pl.BlockSpec(memory_space=pltpu.VMEM),) * 2,
        scratch_shapes=[
            pltpu.VMEM((EOF_PARTS, components * modes // EOF_PARTS, cells), jnp.bfloat16),
            pltpu.VMEM((components * modes // EOF_PARTS, BLK), jnp.float32),
            pltpu.VMEM(((cells // BLK + 1) * height, BLK), jnp.float32),
            pltpu.VMEM((peers, BLK), jnp.int32),
            pltpu.SMEM((peers, BLK), jnp.int32),
            pltpu.SemaphoreType.DMA,
        ],
        compiler_params=pltpu.CompilerParams(vmem_limit_bytes=32 << 20),
        name="remap",
    )(received, eofs)


def from_row(x, to):
    return lax.ppermute(x, "src", [(row, to(row)) for row in range(lax.axis_size("src"))])


def per_device(src_vel, angle, src_block, tgt_block, send_count, intersection, eofs):
    components, rows, cells = src_vel.shape
    src_count = lax.axis_size("src")
    tgt_count = lax.axis_size("tgt")
    cap = src_block.shape[3]
    slots = tgt_count * cap
    blocks = eofs.shape[2] // BLK
    edge = src_vel[:, :, cells - BLK :]
    top = (src_count - 1) * tgt_count
    mirror = lax.ppermute(
        edge, ("src", "tgt"), [(top + t, top + tgt_count - 1 - t) for t in range(tgt_count)]
    )
    src_ids = jnp.swapaxes(src_block, 2, 3).reshape(cap, tgt_count)
    tgt_ids = jnp.swapaxes(tgt_block, 2, 3).reshape(cap, tgt_count)
    counts = send_count.reshape(tgt_count)
    weights = intersection.reshape(slots, BLK, BLK)
    contribs, weights, trig = contributions(
        src_ids, tgt_ids, counts, src_vel, angle, weights, tgt_count
    )
    contribs = fold(contribs, weights, trig, edge, mirror, src_ids)
    received = lax.all_to_all(contribs, "tgt", split_axis=0, concat_axis=0, tiled=True)
    remapped, partial = remap(received, eofs, rows)
    column = jnp.sum(lax.all_to_all(partial, "tgt", 0, 0, tiled=True), axis=0)
    pair = column + from_row(column, lambda row: row ^ 1)
    one, two, three = (
        from_row(pair, lambda row, k=k: (row + 2 * k) % src_count) for k in range(1, src_count // 2)
    )
    total = (pair + two) + (one + three)
    pcs = jnp.concatenate([total[:, :rows], total[:, BLK // 2 : BLK // 2 + rows]], axis=0).T
    return remapped, pcs


def solution(mesh):
    return jax.shard_map(
        per_device,
        mesh=mesh,
        in_specs=(
            P(None, None, ("src", "tgt")),
            P(("src", "tgt")),
            P("src", "tgt", None, None),
            P("src", "tgt", None, None),
            P("src", "tgt", None),
            P("src", "tgt", None, None, None, None),
            P(None, None, ("src", "tgt")),
        ),
        out_specs=(P(None, None, ("src", "tgt")), P(None, "tgt")),
        check_vma=False,
    )
```

```python
import jax
import jax.numpy as jnp
from jax import lax
from jax.experimental import pallas as pl
from jax.experimental.pallas import tpu as pltpu
from jax.sharding import PartitionSpec as P

BLK = 128
ID_ROWS = 8
W_CHUNK = 64
EOF_PARTS = 1


def in_hbm(x):
    return pltpu.with_memory_space_constraint(x, pltpu.HBM)


def contribution_kernel(
    src_ids_hbm,
    tgt_ids_hbm,
    counts_hbm,
    vel_hbm,
    angle_hbm,
    w_hbm,
    out,
    w,
    trig,
    src_ids,
    tgt_ids,
    counts,
    vel,
    angle,
    rot,
    small_sem,
    vel_sem,
    w_sem,
):
    components, rows, cells = vel.shape
    blocks = cells // BLK
    slots = w.shape[0]
    peers, peer_rows, _ = out.shape
    cap = slots // peers
    chunks = slots // W_CHUNK
    height = components * rows

    def w_copy(i):
        part = pl.ds(i * W_CHUNK, W_CHUNK)
        return pltpu.make_async_copy(w_hbm.at[part], w.at[part], w_sem.at[i])

    small = [
        pltpu.make_async_copy(src, dst, small_sem.at[i])
        for i, (src, dst) in enumerate(
            [(src_ids_hbm, src_ids), (tgt_ids_hbm, tgt_ids), (counts_hbm, counts), (angle_hbm, angle)]
        )
    ]
    for copy in small:
        copy.start()
    vel_copy = pltpu.make_async_copy(vel_hbm, vel, vel_sem)
    vel_copy.start()
    for i in range(chunks):
        w_copy(i).start()
    for copy in small:
        copy.wait()
    lane = lax.broadcasted_iota(jnp.int32, (ID_ROWS, BLK), 1)
    for d in range(peers):
        ids = jnp.full((ID_ROWS, BLK), blocks, jnp.int32)
        for j in range(cap):
            ids = jnp.where(lane == j, jnp.where(j < counts[d], tgt_ids[j, d], blocks), ids)
        out[d, cap * height :, :] = ids.astype(jnp.float32).astype(jnp.bfloat16)
    cosine = jnp.cos(angle[...])
    sine = jnp.sin(angle[...])
    trig[0] = cosine
    trig[1] = sine
    vel_copy.wait()
    for b in range(blocks):
        x = vel[0, :, b * BLK : (b + 1) * BLK].astype(jnp.float32)
        y = vel[1, :, b * BLK : (b + 1) * BLK].astype(jnp.float32)
        c = cosine[b : b + 1, :]
        s = sine[b : b + 1, :]
        rot[b, :rows, :] = (c * x - s * y).astype(jnp.bfloat16)
        rot[b, rows:, :] = (s * x + c * y).astype(jnp.bfloat16)

    for d in range(peers):
        if d * cap % W_CHUNK == 0:
            w_copy(d * cap // W_CHUNK).wait()
        for j in range(cap):
            p = d * cap + j
            block = rot[src_ids[j, d]]
            product = jnp.dot(block, w[p], preferred_element_type=jnp.float32)
            out[d, j * height : (j + 1) * height, :] = product.astype(jnp.bfloat16)


def contributions(src_ids, tgt_ids, counts, src_vel, angle, weights, peers):
    components, rows, cells = src_vel.shape
    slots = weights.shape[0]
    blocks = cells // BLK
    height = components * rows
    peer_rows = slots // peers * height + ID_ROWS
    return pl.pallas_call(
        contribution_kernel,
        out_shape=(
            jax.ShapeDtypeStruct((peers, peer_rows, BLK), jnp.bfloat16),
            jax.ShapeDtypeStruct(weights.shape, jnp.bfloat16),
            jax.ShapeDtypeStruct((2, blocks, BLK), jnp.float32),
        ),
        in_specs=[
            pl.BlockSpec(memory_space=pltpu.HBM),
        ]
        * 6,
        out_specs=(pl.BlockSpec(memory_space=pltpu.VMEM),) * 3,
        scratch_shapes=[
            pltpu.SMEM(src_ids.shape, jnp.int32),
            pltpu.SMEM(tgt_ids.shape, jnp.int32),
            pltpu.SMEM(counts.shape, jnp.int32),
            pltpu.VMEM(src_vel.shape, jnp.bfloat16),
            pltpu.VMEM((blocks, BLK), jnp.float32),
            pltpu.VMEM((blocks, height, BLK), jnp.bfloat16),
            pltpu.SemaphoreType.DMA((4,)),
            pltpu.SemaphoreType.DMA,
            pltpu.SemaphoreType.DMA((slots // W_CHUNK,)),
        ],
        compiler_params=pltpu.CompilerParams(vmem_limit_bytes=24 << 20),
        name="contributions",
    )(in_hbm(src_ids), in_hbm(tgt_ids), in_hbm(counts), in_hbm(src_vel), in_hbm(angle.reshape(blocks, BLK)), in_hbm(weights))


def fold_kernel(given, w, trig, edge, mirror, ids_hbm, out, block, ids, sem):
    _, rows, _ = edge.shape
    blocks = trig.shape[1]
    peers = out.shape[0]
    cap = ids.shape[0]
    height = block.shape[0]

    @pl.when(lax.axis_index("src") == lax.axis_size("src") - 1)
    def _():
        copy = pltpu.make_async_copy(ids_hbm, ids, sem)
        copy.start()
        lane = lax.broadcasted_iota(jnp.int32, (BLK, BLK), 0)
        flip = (lane + lax.broadcasted_iota(jnp.int32, (BLK, BLK), 1) == BLK - 1).astype(jnp.float32)
        flip = flip.astype(jnp.bfloat16)
        x, y = (
            0.5 * (edge[c].astype(jnp.float32) - jnp.dot(mirror[c], flip, preferred_element_type=jnp.float32))
            for c in range(2)
        )
        c = trig[0, blocks - 1 : blocks, :]
        s = trig[1, blocks - 1 : blocks, :]
        block[:rows, :] = (c * x - s * y).astype(jnp.bfloat16)
        block[rows:, :] = (s * x + c * y).astype(jnp.bfloat16)
        copy.wait()
        for d in range(peers):
            for j in range(cap):

                @pl.when(ids[j, d] == blocks - 1)
                def _():
                    product = jnp.dot(block[...], w[d * cap + j], preferred_element_type=jnp.float32)
                    out[d, j * height : (j + 1) * height, :] = product.astype(jnp.bfloat16)


def fold(contribs, weights, trig, edge, mirror, src_ids):
    components, rows, _ = edge.shape
    return pl.pallas_call(
        fold_kernel,
        out_shape=jax.ShapeDtypeStruct(contribs.shape, contribs.dtype),
        in_specs=[pl.BlockSpec(memory_space=pltpu.VMEM)] * 5 + [pl.BlockSpec(memory_space=pltpu.HBM)],
        out_specs=pl.BlockSpec(memory_space=pltpu.VMEM),
        scratch_shapes=[
            pltpu.VMEM((components * rows, BLK), jnp.bfloat16),
            pltpu.SMEM(src_ids.shape, jnp.int32),
            pltpu.SemaphoreType.DMA,
        ],
        input_output_aliases={0: 0},
        compiler_params=pltpu.CompilerParams(vmem_limit_bytes=16 << 20),
        name="fold",
    )(contribs, weights, trig, edge, mirror, in_hbm(src_ids))


def remap_kernel(recv, eof_ref, out_ref, pcs_ref, eof, mixed, acc, ids_vmem, ids_smem, sem):
    components, rows, cells = out_ref.shape
    blocks = cells // BLK
    peers, peer_rows, _ = recv.shape
    height = components * rows
    cap = (peer_rows - ID_ROWS) // height
    for s in range(peers):
        ids = recv[s, cap * height : cap * height + ID_ROWS, :].astype(jnp.float32).astype(jnp.int32)
        ids_vmem[s : s + 1, :] = ids[:1, :]
    copy = pltpu.make_async_copy(ids_vmem, ids_smem, sem)
    copy.start()
    modes = eof_ref.shape[0]
    width = modes // EOF_PARTS
    acc[...] = jnp.zeros_like(acc)
    for i in range(EOF_PARTS):
        eof[i] = eof_ref[i * width : (i + 1) * width].reshape(components * width, cells)
    copy.wait()

    def sender(s, carry):
        for j in range(cap):
            start = pl.multiple_of(ids_smem[s, j] * height, height)
            part = recv[s, j * height : (j + 1) * height, :].astype(jnp.float32)
            acc[pl.ds(start, height), :] += part
        return carry

    lax.fori_loop(0, peers, sender, 0, unroll=True)
    for b in range(blocks):
        total = acc[b * height : (b + 1) * height, :].astype(jnp.bfloat16)
        for c in range(components):
            out_ref[c, :, b * BLK : (b + 1) * BLK] = total[c * rows : (c + 1) * rows, :]
    modes = eof_ref.shape[0]
    width = modes // EOF_PARTS
    half = pcs_ref.shape[1]
    pcs_ref[...] = jnp.zeros_like(pcs_ref)
    for i in range(EOF_PARTS):
        product = lax.dot_general(
            out_ref[...].reshape(height, cells),
            eof[i],
            (((1,), (1,)), ((), ())),
            preferred_element_type=jnp.float32,
        )
        mixed[:, :height] = product.T
        result = 0.0
        for c in range(components):
            result += mixed[pl.ds(c, width, stride=components), :][:, c * rows : (c + 1) * rows]
        pieces = result.reshape(width // (2 * half), 2 * half, rows)
        first = i * width // (2 * half)
        pcs_ref[first : first + width // (2 * half), :, :rows] = pieces[:, :half]
        pcs_ref[first : first + width // (2 * half), :, BLK // 2 : BLK // 2 + rows] = pieces[:, half:]


def remap(received, eofs, rows):
    modes, components, cells = eofs.shape
    peers = received.shape[0]
    height = components * rows
    return pl.pallas_call(
        remap_kernel,
        out_shape=(
            jax.ShapeDtypeStruct((components, rows, cells), jnp.bfloat16),
            jax.ShapeDtypeStruct((peers, modes // peers // 2, BLK), jnp.float32),
        ),
        in_specs=[pl.BlockSpec(memory_space=pltpu.VMEM)] * 2,
        out_specs=(pl.BlockSpec(memory_space=pltpu.VMEM),) * 2,
        scratch_shapes=[
            pltpu.VMEM((EOF_PARTS, components * modes // EOF_PARTS, cells), jnp.bfloat16),
            pltpu.VMEM((components * modes // EOF_PARTS, BLK), jnp.float32),
            pltpu.VMEM(((cells // BLK + 1) * height, BLK), jnp.float32),
            pltpu.VMEM((peers, BLK), jnp.int32),
            pltpu.SMEM((peers, BLK), jnp.int32),
            pltpu.SemaphoreType.DMA,
        ],
        compiler_params=pltpu.CompilerParams(vmem_limit_bytes=32 << 20),
        name="remap",
    )(received, eofs)


def from_row(x, to):
    return lax.ppermute(x, "src", [(row, to(row)) for row in range(lax.axis_size("src"))])


def per_device(src_vel, angle, src_block, tgt_block, send_count, intersection, eofs):
    components, rows, cells = src_vel.shape
    src_count = lax.axis_size("src")
    tgt_count = lax.axis_size("tgt")
    cap = src_block.shape[3]
    slots = tgt_count * cap
    blocks = eofs.shape[2] // BLK
    edge = src_vel[:, :, cells - BLK :]
    top = (src_count - 1) * tgt_count
    mirror = lax.ppermute(
        edge, ("src", "tgt"), [(top + t, top + tgt_count - 1 - t) for t in range(tgt_count)]
    )
    src_ids = jnp.swapaxes(src_block, 2, 3).reshape(cap, tgt_count)
    tgt_ids = jnp.swapaxes(tgt_block, 2, 3).reshape(cap, tgt_count)
    counts = send_count.reshape(tgt_count)
    weights = intersection.reshape(slots, BLK, BLK)
    contribs, weights, trig = contributions(
        src_ids, tgt_ids, counts, src_vel, angle, weights, tgt_count
    )
    contribs = fold(contribs, weights, trig, edge, mirror, src_ids)
    received = lax.all_to_all(contribs, "tgt", split_axis=0, concat_axis=0, tiled=True)
    remapped, partial = remap(received, eofs, rows)
    column = jnp.sum(lax.all_to_all(partial, "tgt", 0, 0, tiled=True), axis=0)
    pair = column + from_row(column, lambda row: row ^ 1)
    one, two, three = (
        from_row(pair, lambda row, k=k: (row + 2 * k) % src_count) for k in range(1, src_count // 2)
    )
    total = (pair + two) + (one + three)
    pcs = jnp.concatenate([total[:, :rows], total[:, BLK // 2 : BLK // 2 + rows]], axis=0).T
    return remapped, pcs


def solution(mesh):
    return jax.shard_map(
        per_device,
        mesh=mesh,
        in_specs=(
            P(None, None, ("src", "tgt")),
            P(("src", "tgt")),
            P("src", "tgt", None, None),
            P("src", "tgt", None, None),
            P("src", "tgt", None),
            P("src", "tgt", None, None, None, None),
            P(None, None, ("src", "tgt")),
        ),
        out_specs=(P(None, None, ("src", "tgt")), P(None, "tgt")),
        check_vma=False,
    )
```
